128 devices in a mesh: pop: 8 (over x, core), fsdp: 16 (over y, z).
Axes of the slice: x: 4, y: 4, z: 4, core: 2. Of those that a mesh axis runs over, the one named last changes fastest.
Arguments:
- tokens: bfloat16 [2048, 5120], P('pop', 'fsdp'), may hold values from -6 to 6
- seeds: int32 [2048], replicated, may hold values from 0 to 1048575
- fitness: float32 [2048], P(('pop', 'fsdp')), may hold values from -60 to 60
- gate_weight: bfloat16 [5120, 14336], P('fsdp', 'pop'), may hold values from -0.078125 to 0.078125
- up_weight: bfloat16 [5120, 14336], P('fsdp', 'pop'), may hold values from -0.078125 to 0.078125
- gate_first: float32 [5120, 14336], P('fsdp', 'pop'), may hold values from -4 to 4
- up_first: float32 [5120, 14336], P('fsdp', 'pop'), may hold values from -4 to 4
- gate_second: float32 [5120, 14336], P('fsdp', 'pop'), may hold values from 0.05 to 2
- up_second: float32 [5120, 14336], P('fsdp', 'pop'), may hold values from 0.05 to 2
Outputs:
- hidden: bfloat16 [2048, 14336], P('fsdp', 'pop')
- gate_new: bfloat16 [5120, 14336], P('fsdp', 'pop')
- up_new: bfloat16 [5120, 14336], P('fsdp', 'pop')
- gate_first_new: float32 [5120, 14336], P('fsdp', 'pop')
- up_first_new: float32 [5120, 14336], P('fsdp', 'pop')
- gate_second_new: float32 [5120, 14336], P('fsdp', 'pop')
- up_second_new: float32 [5120, 14336], P('fsdp', 'pop')
The draws below stay inside these ranges and needn't reach their ends.
All inputs are finite; a program needn't handle non-finite values.
Results may differ from the reference program's by a relative error of at most 0.0022.
Values may be sent and summed in bfloat16 or wider, within the bound.
A program may use at most 128 MiB of HBM per device.

```python
import math
import jax
import jax.numpy as jnp
from jax import lax

D = 5120
FW = 14336
MEMBERS = 2048


def draw_fitness(key, part):
    order = jnp.arange(MEMBERS, dtype=jnp.float32) / (MEMBERS - 1)
    noise = jax.random.truncated_normal(jax.random.fold_in(key, 23), -4.0, 4.0, (MEMBERS,), jnp.float32)
    spread = jnp.exp(order * math.log(10.0))
    return (spread * noise + 0.5 + 1.5 * order).astype(jnp.float32)


def plant(entries, stream_key, smallest, top_value):
    longest = entries.shape.index(max(entries.shape))
    spots = []
    for shift in (0, 1):
        where = [jax.random.randint(jax.random.fold_in(stream_key, axis), (), 0, length) for axis, length in enumerate(entries.shape)]
        where[longest] = (where[longest] + shift) % entries.shape[longest]
        spots.append(tuple(where))
    return entries.at[spots[0]].set(smallest).at[spots[1]].set(top_value)


def shard_levels(rng, shape, pieces, smallest, high):
    factor_of = 1.0
    for axis_at, parts in pieces:
        steps = jax.random.uniform(jax.random.fold_in(jax.random.fold_in(rng, 6), axis_at), (parts,), jnp.float32, smallest / len(pieces), high / len(pieces))
        factor_of = factor_of * jnp.repeat(jnp.exp(steps), shape[axis_at] // parts).reshape((-1,) + (1,) * (len(shape) - 1 - axis_at))
    return factor_of


def scatter_about(key, dims, scale, most, cuts=(), held_as=jnp.bfloat16):
    drawn = jax.random.normal(key, dims, jnp.float32) * scale
    if len(cuts) > 0:
        drawn = shard_levels(key, dims, cuts, -0.22, 0.18) * drawn
    return jnp.clip(drawn, min=-most, max=most).astype(held_as)


def setup_inputs(seed: int = 0) -> dict:
    key_list = jax.random.split(jax.random.key(seed), 10)
    return {
        "tokens": scatter_about(key_list[0], (MEMBERS, D), 1.0, 6.0, ((0, 8), (1, 16))),
        "seeds": plant(jax.random.randint(key_list[1], (MEMBERS,), 0, 1048576), jax.random.fold_in(key_list[1], 1), 0, 1048575).astype(jnp.int32),
        "fitness": draw_fitness(jax.random.fold_in(key_list[9], 71), 0),
        "gate_weight": scatter_about(key_list[3], (D, FW), D ** -0.5, 0.078125, ((0, 16), (1, 8))),
        "up_weight": scatter_about(key_list[4], (D, FW), D ** -0.5, 0.078125, ((0, 16), (1, 8))),
        "gate_first": scatter_about(key_list[5], (D, FW), 0.5, 4.0, ((0, 16), (1, 8)), jnp.float32),
        "up_first": scatter_about(key_list[6], (D, FW), 0.5, 4.0, ((0, 16), (1, 8)), jnp.float32),
        "gate_second": jnp.clip(jnp.exp(math.log(2.0) - 3.6888794 * jax.random.uniform(key_list[7], (D, FW), jnp.float32) ** shard_levels(key_list[7], (D, FW), ((0, 16), (1, 8)), -0.2, 0.2)), 0.05, 2.0),
        "up_second": jnp.clip(jnp.exp(math.log(2.0) - 3.6888794 * jax.random.uniform(key_list[8], (D, FW), jnp.float32) ** shard_levels(key_list[8], (D, FW), ((0, 16), (1, 8)), -0.2, 0.2)), 0.05, 2.0),
    }


noise_scale = 0.01
learn_rate = 0.002
beta_first = 0.9
beta_second = 0.99
adam_floor = 1e-08
stat_epsilon = 1e-06

def factor_block(seeds, start, count, salt):
    columns = jnp.arange(count, dtype=jnp.int32) + start
    mixed = seeds[:, None] * 1103515245 + columns[None, :] * 40503 + salt * 7919
    mixed = jnp.bitwise_xor(mixed, jnp.right_shift(mixed, 15))
    mixed = mixed * 73244475
    mixed = jnp.bitwise_xor(mixed, jnp.right_shift(mixed, 13))
    level = jnp.bitwise_and(mixed, 255)
    return ((2 * level - 255).astype(jnp.float32) * (1.0 / 256.0)).astype(jnp.bfloat16)

def perturbed(tokens, weight, left, right):
    base = jnp.dot(tokens, weight, preferred_element_type=jnp.float32)
    along = lax.optimization_barrier(jnp.sum(tokens.astype(jnp.float32) * left.astype(jnp.float32), axis=1))
    return base + noise_scale * along[:, None] * right.astype(jnp.float32)

def gradient(scaled, left, right):
    weighted = (scaled[:, None] * right.astype(jnp.float32)).astype(jnp.bfloat16)
    total = lax.dot_general(left, weighted, (((0,), (0,)), ((), ())), preferred_element_type=jnp.float32)
    return total * (1.0 / (left.shape[0] * noise_scale))

def adam_step(weight, first, second, grad):
    first_new = beta_first * first + (1.0 - beta_first) * grad
    second_new = beta_second * second + (1.0 - beta_second) * grad * grad
    moved = weight.astype(jnp.float32) + learn_rate * first_new / (jnp.sqrt(second_new) + adam_floor)
    return (moved.astype(jnp.bfloat16), first_new, second_new)

def reference(tokens, seeds, fitness, gate_weight, up_weight, gate_first, up_first, gate_second, up_second):
    left_gate = factor_block(seeds, 0, D, 1)
    right_gate = factor_block(seeds, 0, FW, 2)
    left_up = factor_block(seeds, 0, D, 3)
    right_up = factor_block(seeds, 0, FW, 4)
    gate = perturbed(tokens, gate_weight, left_gate, right_gate)
    up = perturbed(tokens, up_weight, left_up, right_up)
    hidden = (jax.nn.silu(gate) * up).astype(jnp.bfloat16)
    center = jnp.mean(fitness)
    spread = jnp.mean(jnp.square(fitness - center))
    scaled = (fitness - center) / jnp.sqrt(spread + stat_epsilon)
    grad_gate = gradient(scaled, left_gate, right_gate)
    grad_up = gradient(scaled, left_up, right_up)
    gate_new, gate_first_new, gate_second_new = adam_step(gate_weight, gate_first, gate_second, grad_gate)
    up_new, up_first_new, up_second_new = adam_step(up_weight, up_first, up_second, grad_up)
    return (hidden, gate_new, up_new, gate_first_new, up_first_new, gate_second_new, up_second_new)
```

```python
import functools

import jax
import jax.numpy as jnp
from jax import lax
from jax.experimental import pallas as pl
from jax.experimental.pallas import tpu as pltpu
from jax.sharding import PartitionSpec as P

MESH = pl.DeviceIdType.MESH

noise_scale = 0.01
learn_rate = 0.002
beta_first = 0.9
beta_second = 0.99
adam_floor = 1e-08
stat_epsilon = 1e-06

MEMBERS = 2048
SEED_STEP = 1103515245
COLUMN_STEP = 40503
SALT_STEP = 7919
MIX = 73244475
LEVELS = 32767.0
ROUNDER = 12582912.0


def levels_of(mixed):
    mixed = mixed ^ (mixed >> 15)
    mixed = mixed * MIX
    mixed = mixed ^ (mixed >> 13)
    return (mixed & 255).astype(jnp.float32) - 127.5


def column_of(row, eye):
    return jnp.sum(jnp.where(eye, row, 0.0), axis=1, keepdims=True)


def row_of(column, eye):
    return jnp.sum(jnp.where(eye, column, 0.0), axis=0, keepdims=True)


def remote(src, dst, send_sem, recv_sem, device):
    return pltpu.make_async_remote_copy(
        src_ref=src,
        dst_ref=dst,
        send_sem=send_sem,
        recv_sem=recv_sem,
        device_id=device,
        device_id_type=MESH,
    )


def place(x, c, y, z):
    return {"pop": 2 * lax.rem(x, 4) + c, "fsdp": 4 * lax.rem(y, 4) + lax.rem(z, 4)}


def kernel(
    tokens,
    seeds,
    fitness,
    gate_w,
    up_w,
    hidden,
    grad_gate,
    grad_up,
    xg,
    xk,
    wx,
    info,
    seed_mul,
    scaled,
    ps,
    sc,
    pr,
    sr,
    p0,
    lt,
    wt,
    gb,
    hs,
    ho,
    s_xz,
    r_xz,
    s_xx,
    r_xx,
    l_x,
    s_w,
    r_w,
    s_c,
    r_c,
    s_i,
    r_i,
    s_ic,
    r_ic,
    s_p,
    r_p,
    s_q,
    r_q,
    s_h,
    r_h,
    l_g,
):
    pop = lax.axis_index("pop")
    fsdp = lax.axis_index("fsdp")
    x, c = pop // 2, pop % 2
    y, z = fsdp // 4, fsdp % 4
    width = tokens.shape[1]
    half = wx.shape[3]
    units = 2 * half
    z_core, z_half = z // 2, z % 2
    partner = place(x, 1 - c, y, z)

    barrier = pltpu.get_barrier_semaphore()
    for dc in range(2):
        for dz in range(4):
            if dc or dz:
                pl.semaphore_signal(
                    barrier,
                    inc=1,
                    device_id=place(x, (c + dc) % 2, y, z + dz),
                    device_id_type=MESH,
                )
    for d in range(1, 4):
        pl.semaphore_signal(barrier, inc=1, device_id=place(x + d, c, y, z), device_id_type=MESH)
        pl.semaphore_signal(barrier, inc=1, device_id=place(x, c, y + d, z), device_id_type=MESH)
    pl.semaphore_wait(barrier, 13)

    for d in (1, 3, 2):
        remote(tokens, xg.at[x, z], s_xz.at[d - 1], r_xz.at[d - 1], place(x, c, y, z + d)).start()
    for d in (1, 3, 2):
        remote(
            tokens, xg.at[x, z], s_xx.at[d - 1, 0], r_xx.at[d - 1, 0], place(x + d, c, y, z)
        ).start()
    own = pltpu.make_async_copy(tokens, xg.at[x, z], l_x)
    own.start()

    def weight_send(cm, h):
        src = (gate_w, up_w)[cm].at[:, pl.ds(h * half, half)]
        mine = jnp.logical_and(c == cm, 2 * c + h == z)
        away = remote(
            src, wx.at[cm, z], s_w.at[2 * cm + h], r_w.at[z], place(x, cm, y, 2 * c + h)
        )
        here = pltpu.make_async_copy(src, wx.at[cm, z], r_w.at[z])
        return mine, away, here

    for h in range(2):
        for cm in range(2):
            mine, away, here = weight_send(cm, h)
            pl.when(jnp.logical_not(mine))(away.start)
            pl.when(mine)(here.start)

    eye = lax.broadcasted_iota(jnp.int32, (128, 128), 0) == lax.broadcasted_iota(
        jnp.int32, (128, 128), 1
    )
    seed_mul[...] = seeds[...] * SEED_STEP
    my_info = info.at[c, y, x, z]
    my_info[...] = fitness[...]
    left_columns = (
        lax.broadcasted_iota(jnp.int32, (1, width), 1) + fsdp * width
    ) * COLUMN_STEP
    for b in range(2):
        seed_row = seeds[pl.ds(2 * pop + b, 1), :].astype(jnp.float32)
        seed_col = column_of(seed_row, eye).astype(jnp.int32) * SEED_STEP
        rows = tokens[b * 128 : (b + 1) * 128, :].astype(jnp.float32)
        for k, salt in ((0, 1), (1, 3)):
            left = levels_of(seed_col + (left_columns + salt * SALT_STEP))
            along = jnp.sum(rows * left, axis=1, keepdims=True) * (1.0 / 128.0)
            my_info[1 + 2 * k + b : 2 + 2 * k + b, :] = row_of(along, eye)

    def info_send(stage, ref, d, device):
        return remote(ref, ref, s_i.at[stage, d - 1], r_i.at[stage, d - 1], device)

    for d in range(1, 4):
        info_send(0, info.at[c, y, x, z], d, place(x, c, y, z + d)).start()

    def forward(j):
        piece = xg.at[x, lax.rem(z + 4 - j, 4)]
        remote(piece, piece, s_xz.at[j - 1], r_xz.at[j - 1], place(x, c, y, z + j)).wait_recv()
        for d in (1, 3, 2):
            remote(
                piece, piece, s_xx.at[d - 1, j], r_xx.at[d - 1, j], place(x + d, c, y, z)
            ).start()

    def info_arrived(stage, ref_of):
        for d in range(1, 4):
            info_send(stage, ref_of(d), d, partner).wait_recv()

    for j in (1, 3, 2):
        forward(j)
    info_arrived(0, lambda d: info.at[c, y, x, lax.rem(z + 4 - d, 4)])
    for d in range(1, 4):
        info_send(1, info.at[c, y, x], d, place(x + d, c, y, z)).start()

    sub = lax.broadcasted_iota(jnp.int32, (32, 128), 0)

    def fill_left(k, salt):
        def body(i, _):
            term = (sub + (fsdp * width + i * 32)) * COLUMN_STEP + salt * SALT_STEP
            at = pl.ds(pl.multiple_of(i * 32, 32), 32)
            for r in range(16):
                lt[k, at, r * 128 : (r + 1) * 128] = levels_of(
                    seed_mul[r : r + 1, :] + term
                ).astype(jnp.bfloat16)
            return 0

        lax.fori_loop(0, width // 32, body, 0)

    fill_left(0, 1)
    info_arrived(1, lambda d: info.at[c, y, lax.rem(x + 4 - d, 4)])
    for d in range(1, 4):
        info_send(2, info.at[c, y], d, place(x, c, y + d, z)).start()
    fill_left(1, 3)
    info_arrived(2, lambda d: info.at[c, lax.rem(y + 4 - d, 4)])
    remote(info.at[c], info.at[c], s_ic, r_ic, partner).start()
    remote(info.at[1 - c], info.at[1 - c], s_ic, r_ic, partner).wait_recv()

    lane = lax.broadcasted_iota(jnp.int32, (1, 128), 1) // 16
    for r in range(16):
        p, k = r // 2, r % 2
        row = jnp.zeros((1, 128), jnp.float32)
        for s in range(8):
            tile = info[p % 2, 2 * k + s // 4, p // 2, s % 4, 0:1, :]
            row = jnp.where(lane == s, tile, row)
        scaled[r : r + 1, :] = row
    whole = scaled[...]
    center = jnp.sum(jnp.sum(whole, axis=1, keepdims=True), axis=0, keepdims=True) / MEMBERS
    apart = whole - center
    spread = (
        jnp.sum(jnp.sum(apart * apart, axis=1, keepdims=True), axis=0, keepdims=True) / MEMBERS
    )
    scaled[...] = apart / jnp.sqrt(spread + stat_epsilon)

    chunk = wt.shape[0]

    def gradient(k, salt, first, last):
        def body(i, _):
            def fill(q, _):
                term = (sub + (pop * units + i * chunk + q * 32)) * COLUMN_STEP + salt * SALT_STEP
                at = pl.ds(pl.multiple_of(q * 32, 32), 32)
                for r in range(16):
                    wt[at, r * 128 : (r + 1) * 128] = (
                        levels_of(seed_mul[r : r + 1, :] + term) * scaled[r : r + 1, :]
                    ).astype(jnp.bfloat16)
                return 0

            lax.fori_loop(0, chunk // 32, fill, 0)
            total = lax.dot_general(
                lt[k], wt[...], (((1,), (1,)), ((), ())), preferred_element_type=jnp.float32
            )
            gb[k, :, pl.ds(pl.multiple_of(i * chunk, chunk), chunk)] = total * (
                1.0 / (MEMBERS * noise_scale) / 16384.0
            )
            return 0

        lax.fori_loop(first, last, body, 0)

    chunks = units // chunk
    gradient(0, 2, 0, chunks)
    copy_gate = pltpu.make_async_copy(gb.at[0], grad_gate, l_g.at[0])
    copy_gate.start()
    gradient(1, 4, 0, 2)

    for s in range(4):
        remote(wx.at[c, s], wx.at[c, s], s_w.at[0], r_w.at[s], partner).wait_recv()
        remote(wx.at[c, s], wx.at[c, s], s_c.at[s], r_c.at[s], partner).start()
    own.wait()
    for j in range(4):
        for d in range(1, 4):
            piece = xg.at[lax.rem(x + 4 - d, 4), lax.rem(z + 4 - j, 4)]
            remote(
                piece, piece, s_xx.at[d - 1, j], r_xx.at[d - 1, j], place(x + d, c, y, z)
            ).wait_recv()
    for s in range(4):
        xk[s] = jnp.concatenate([xg[s, j] for j in range(4)], axis=1)
    for s in range(4):
        remote(wx.at[1 - c, s], wx.at[1 - c, s], s_c.at[s], r_c.at[s], partner).wait_recv()

    for d in (2, 1, 3, 0):
        to = lax.rem(y + d, 4)
        rows = xk[to]
        for k in range(2):
            p0[:, k * half : (k + 1) * half] = jnp.dot(
                rows, wx[k].reshape(4 * width, half), preferred_element_type=jnp.float32
            )
        if d == 0:
            break
        for b in range(2):
            at = slice(b * 128, (b + 1) * 128)
            for k in range(2):
                over = slice(k * half, (k + 1) * half)
                top = jnp.max(jnp.abs(p0[at, over]), axis=1, keepdims=True)
                top = jnp.maximum(top, 1e-30)
                grown = p0[at, over] * (LEVELS / top)
                whole_number = (grown + ROUNDER) - ROUNDER
                ps[d - 1, at, over] = whole_number.astype(jnp.int32).astype(jnp.int16)
                sc[d - 1, 2 * k + b : 2 * k + b + 1, :] = row_of(top * (1.0 / LEVELS), eye)
        there = place(x, c, y + d, z)
        remote(ps.at[d - 1], pr.at[d - 1], s_p.at[d - 1], r_p.at[d - 1], there).start()
        remote(sc.at[d - 1], sr.at[d - 1], s_q.at[d - 1], r_q.at[d - 1], there).start()

    gradient(1, 4, 2, chunks)
    copy_up = pltpu.make_async_copy(gb.at[1], grad_up, l_g.at[1])
    copy_up.start()

    for d in (1, 3, 2):
        remote(ps.at[d - 1], pr.at[d - 1], s_p.at[d - 1], r_p.at[d - 1], partner).wait_recv()
        remote(sc.at[d - 1], sr.at[d - 1], s_q.at[d - 1], r_q.at[d - 1], partner).wait_recv()

    first_unit = (2 * x + z_core) * units + z_half * half
    for b in range(2):
        at = slice(b * 128, (b + 1) * 128)
        seed_row = seeds[pl.ds(2 * (2 * y + c) + b, 1), :].astype(jnp.float32)
        seed_col = column_of(seed_row, eye).astype(jnp.int32) * SEED_STEP
        along = []
        for k in range(2):
            row = jnp.zeros((1, 128), jnp.float32)
            for yy in range(4):
                for zz in range(4):
                    row = row + info[c, yy, y, zz, 1 + 2 * k + b : 2 + 2 * k + b, :]
            along.append(column_of(row, eye) * noise_scale)
        steps = [
            [column_of(sr[d, 2 * k + b : 2 * k + b + 1, :], eye) for d in range(3)]
            for k in range(2)
        ]

        def finish(j, _):
            out = []
            for k, salt in ((0, 2), (1, 4)):
                over = pl.ds(pl.multiple_of(k * half + j * 128, 128), 128)
                total = p0[at, over]
                for d in range(3):
                    total = total + pr[d, at, over].astype(jnp.int32).astype(
                        jnp.float32
                    ) * steps[k][d]
                columns = (
                    lax.broadcasted_iota(jnp.int32, (1, 128), 1) + (first_unit + j * 128)
                ) * COLUMN_STEP + salt * SALT_STEP
                right = levels_of(seed_col + columns) * (1.0 / 128.0)
                out.append(total + along[k] * right)
            gate, up = out
            value = gate / (1.0 + jnp.exp(-gate)) * up
            hs[b, :, pl.ds(pl.multiple_of(j * 128, 128), 128)] = value.astype(jnp.bfloat16)
            return 0

        lax.fori_loop(0, half // 128, finish, 0)
        mine = jnp.logical_and(z_core == c, 2 * c + b == z)
        away = remote(
            hs.at[b], ho.at[z_half], s_h.at[b], r_h.at[z_half], place(x, z_core, y, 2 * c + b)
        )
        here = pltpu.make_async_copy(hs.at[b], ho.at[z_half], r_h.at[z_half])
        pl.when(jnp.logical_not(mine))(away.start)
        pl.when(mine)(here.start)

    for h in range(2):
        remote(ho.at[h], ho.at[h], s_h.at[0], r_h.at[h], partner).wait_recv()
        hidden[:, h * half : (h + 1) * half] = ho[h]

    for d in range(1, 4):
        remote(tokens, xg.at[x, z], s_xz.at[d - 1], r_xz.at[d - 1], partner).wait_send()
        for j in range(4):
            remote(tokens, xg.at[x, z], s_xx.at[d - 1, j], r_xx.at[d - 1, j], partner).wait_send()
        info_send(0, info.at[c, y, x, z], d, partner).wait_send()
        info_send(1, info.at[c, y, x], d, partner).wait_send()
        info_send(2, info.at[c, y], d, partner).wait_send()
        remote(ps.at[d - 1], pr.at[d - 1], s_p.at[d - 1], r_p.at[d - 1], partner).wait_send()
        remote(sc.at[d - 1], sr.at[d - 1], s_q.at[d - 1], r_q.at[d - 1], partner).wait_send()
    remote(info.at[c], info.at[c], s_ic, r_ic, partner).wait_send()
    for h in range(2):
        for cm in range(2):
            mine, away, here = weight_send(cm, h)
            pl.when(jnp.logical_not(mine))(away.wait_send)
    for s in range(4):
        remote(wx.at[c, s], wx.at[c, s], s_c.at[s], r_c.at[s], partner).wait_send()
    for b in range(2):
        mine = jnp.logical_and(z_core == c, 2 * c + b == z)
        away = remote(
            hs.at[b], ho.at[z_half], s_h.at[b], r_h.at[z_half], place(x, z_core, y, 2 * c + b)
        )
        pl.when(jnp.logical_not(mine))(away.wait_send)
    copy_gate.wait()
    copy_up.wait()


def adam_step(weight, first, second, grad):
    first_new = beta_first * first + (1.0 - beta_first) * grad
    second_new = beta_second * second + (1.0 - beta_second) * grad * grad
    moved = weight.astype(jnp.float32) + learn_rate * first_new / (
        jnp.sqrt(second_new) + adam_floor
    )
    return (moved.astype(jnp.bfloat16), first_new, second_new)


def shards(
    tokens, seeds, fitness, gate_weight, up_weight, gate_first, up_first, gate_second, up_second
):
    width, units = gate_weight.shape
    half = units // 2
    rows = tokens.shape[0]
    bf, f32, i32, i16 = jnp.bfloat16, jnp.float32, jnp.int32, jnp.int16
    vmem = pl.BlockSpec(memory_space=pltpu.VMEM)
    anywhere = pl.BlockSpec(memory_space=pl.ANY)
    dma = pltpu.SemaphoreType.DMA
    tile = jnp.broadcast_to(jnp.tile(fitness, 8)[None], (8, 128))
    hidden, grad_gate, grad_up = pl.pallas_call(
        kernel,
        name="generation",
        out_shape=(
            jax.ShapeDtypeStruct((rows // 2, units), bf),
            jax.ShapeDtypeStruct((width, units), f32),
            jax.ShapeDtypeStruct((width, units), f32),
        ),
        in_specs=[vmem, vmem, vmem, anywhere, anywhere],
        out_specs=(vmem, anywhere, anywhere),
        scratch_shapes=[
            pltpu.VMEM((4, 4, rows, width), bf),
            pltpu.VMEM((4, rows, 4 * width), bf),
            pltpu.VMEM((2, 4, width, half), bf),
            pltpu.VMEM((2, 4, 4, 4, 8, 128), f32),
            pltpu.VMEM((16, 128), i32),
            pltpu.VMEM((16, 128), f32),
            pltpu.VMEM((3, rows, units), i16),
            pltpu.VMEM((3, 8, 128), f32),
            pltpu.VMEM((3, rows, units), i16),
            pltpu.VMEM((3, 8, 128), f32),
            pltpu.VMEM((rows, units), f32),
            pltpu.VMEM((2, width, MEMBERS), bf),
            pltpu.VMEM((256, MEMBERS), bf),
            pltpu.VMEM((2, width, units), f32),
            pltpu.VMEM((2, rows // 2, half), bf),
            pltpu.VMEM((2, rows // 2, half), bf),
            dma((3,)),
            dma((3,)),
            dma((3, 4)),
            dma((3, 4)),
            dma,
            dma((4,)),
            dma((4,)),
            dma((4,)),
            dma((4,)),
            dma((3, 3)),
            dma((3, 3)),
            dma,
            dma,
            dma((3,)),
            dma((3,)),
            dma((3,)),
            dma((3,)),
            dma((2,)),
            dma((2,)),
            dma((2,)),
        ],
        compiler_params=pltpu.CompilerParams(
            collective_id=0, has_side_effects=True, vmem_limit_bytes=56 << 20
        ),
    )(tokens, seeds.reshape(16, 128), tile, gate_weight, up_weight)
    gate_new, gate_first_new, gate_second_new = adam_step(
        gate_weight, gate_first, gate_second, grad_gate
    )
    up_new, up_first_new, up_second_new = adam_step(up_weight, up_first, up_second, grad_up)
    return (hidden, gate_new, up_new, gate_first_new, up_first_new, gate_second_new, up_second_new)


def solution(mesh):
    spread = P("fsdp", "pop")
    return jax.shard_map(
        shards,
        mesh=mesh,
        in_specs=(P("pop", "fsdp"), P(), P(("pop", "fsdp"))) + (spread,) * 6,
        out_specs=(spread,) * 7,
        check_vma=False,
    )
```

```python
import functools

import jax
import jax.numpy as jnp
from jax import lax
from jax.experimental import pallas as pl
from jax.experimental.pallas import tpu as pltpu
from jax.sharding import PartitionSpec as P

MESH = pl.DeviceIdType.MESH

noise_scale = 0.01
learn_rate = 0.002
beta_first = 0.9
beta_second = 0.99
adam_floor = 1e-08
stat_epsilon = 1e-06

MEMBERS = 2048
SEED_STEP = 1103515245
COLUMN_STEP = 40503
SALT_STEP = 7919
MIX = 73244475
LEVELS = 32767.0
EARLY = 3
ROUNDER = 12582912.0


def levels_of(mixed):
    mixed = mixed ^ (mixed >> 15)
    mixed = mixed * MIX
    mixed = mixed ^ (mixed >> 13)
    return (mixed & 255).astype(jnp.float32) - 127.5


def column_of(row, eye):
    return jnp.sum(jnp.where(eye, row, 0.0), axis=1, keepdims=True)


def row_of(column, eye):
    return jnp.sum(jnp.where(eye, column, 0.0), axis=0, keepdims=True)


def remote(src, dst, send_sem, recv_sem, device):
    return pltpu.make_async_remote_copy(
        src_ref=src,
        dst_ref=dst,
        send_sem=send_sem,
        recv_sem=recv_sem,
        device_id=device,
        device_id_type=MESH,
    )


def place(x, c, y, z):
    return {"pop": 2 * lax.rem(x, 4) + c, "fsdp": 4 * lax.rem(y, 4) + lax.rem(z, 4)}


def kernel(
    tokens,
    seeds,
    fitness,
    gate_w,
    up_w,
    hidden,
    grad_gate,
    grad_up,
    xg,
    xk,
    wx,
    info,
    seed_mul,
    scaled,
    ps,
    sc,
    pr,
    sr,
    fs,
    fq,
    fr,
    fp,
    p0,
    lt,
    wt,
    gb,
    hs,
    ho,
    s_xz,
    r_xz,
    s_xx,
    r_xx,
    s_xr,
    r_xr,
    l_x,
    s_w,
    r_w,
    s_c,
    r_c,
    s_i,
    r_i,
    s_ic,
    r_ic,
    s_p,
    r_p,
    s_q,
    r_q,
    s_f,
    r_f,
    s_g,
    r_g,
    s_h,
    r_h,
    l_g,
):
    pop = lax.axis_index("pop")
    fsdp = lax.axis_index("fsdp")
    x, c = pop // 2, pop % 2
    y, z = fsdp // 4, fsdp % 4
    width = tokens.shape[0]
    half = wx.shape[4]
    units = 2 * half
    z_core, z_half = z // 2, z % 2
    split = width // 2
    partner = place(x, 1 - c, y, z)

    barrier = pltpu.get_barrier_semaphore()
    for dc in range(2):
        for dz in range(4):
            if dc or dz:
                pl.semaphore_signal(
                    barrier,
                    inc=1,
                    device_id=place(x, (c + dc) % 2, y, z + dz),
                    device_id_type=MESH,
                )
    for d in range(1, 4):
        pl.semaphore_signal(barrier, inc=1, device_id=place(x + d, c, y, z), device_id_type=MESH)
        pl.semaphore_signal(barrier, inc=1, device_id=place(x, c, y + d, z), device_id_type=MESH)
    pl.semaphore_wait(barrier, 13)

    for d in (1, 3, 2):
        remote(tokens, xg.at[x, z], s_xz.at[d - 1], r_xz.at[d - 1], place(x, c, y, z + d)).start()
    for way in range(2):
        remote(
            tokens,
            xg.at[x, z],
            s_xx.at[way, 0],
            r_xx.at[way, 0],
            place(x + 1 + 2 * way, c, y, z),
        ).start()
    own = pltpu.make_async_copy(tokens, xg.at[x, z], l_x)
    own.start()

    eye = lax.broadcasted_iota(jnp.int32, (128, 128), 0) == lax.broadcasted_iota(
        jnp.int32, (128, 128), 1
    )
    seed_mul[...] = seeds[...] * SEED_STEP
    my_info = info.at[c, y, x, z]
    my_info[...] = fitness[...]
    sub = lax.broadcasted_iota(jnp.int32, (32, 128), 0)
    own.wait()
    for b in range(2):
        seed_row = seeds[pl.ds(2 * pop + b, 1), :] * SEED_STEP

        def add_along(i, sums):
            at = pl.ds(pl.multiple_of(i * 32, 32), 32)
            rows = xg[x, z, at, b * 128 : (b + 1) * 128].astype(jnp.float32)
            term = (sub + (fsdp * width + i * 32)) * COLUMN_STEP
            return tuple(
                kept + rows * levels_of(seed_row + (term + salt * SALT_STEP))
                for kept, salt in zip(sums, (1, 3))
            )

        zero = jnp.zeros((32, 128), jnp.float32)
        sums = lax.fori_loop(0, width // 32, add_along, (zero, zero))
        for k in range(2):
            my_info[1 + 2 * k + b : 2 + 2 * k + b, :] = jnp.sum(
                sums[k], axis=0, keepdims=True
            ) * (1.0 / 128.0)

    def info_send(stage, ref, d, device):
        return remote(ref, ref, s_i.at[stage, d - 1], r_i.at[stage, d - 1], device)

    for d in range(1, 4):
        info_send(0, info.at[c, y, x, z], d, place(x, c, y, z + d)).start()

    def piece_of(source, j):
        return xg.at[lax.rem(source, 4), lax.rem(z + 4 - j, 4)]

    def over_x(piece, way, j):
        there = place(x + 1 + 2 * way, c, y, z)
        return remote(piece, piece, s_xx.at[way, j], r_xx.at[way, j], there)

    def half_over_x(source, way, j):
        piece = piece_of(source, j).at[way * split : (way + 1) * split]
        there = place(x + 1 + 2 * way, c, y, z)
        return remote(piece, piece, s_xr.at[way, j], r_xr.at[way, j], there)

    def forward(j):
        piece = piece_of(x, j)
        remote(piece, piece, s_xz.at[j - 1], r_xz.at[j - 1], place(x, c, y, z + j)).wait_recv()
        for way in range(2):
            over_x(piece, way, j).start()

    def relay(j):
        for way in range(2):
            source = x + 3 - 2 * way
            over_x(piece_of(source, j), way, j).wait_recv()
            half_over_x(source, way, j).start()

    def info_arrived(stage, ref_of):
        for d in range(1, 4):
            info_send(stage, ref_of(d), d, partner).wait_recv()

    def weight_send(k, h, r):
        src = (gate_w, up_w)[k].at[r * split : (r + 1) * split, h * half : (h + 1) * half]
        mine = jnp.logical_and(c == r, 2 * c + h == z)
        away = remote(
            src, wx.at[k, z, r], s_w.at[k, 2 * h + r], r_w.at[k, z], place(x, r, y, 2 * c + h)
        )
        here = pltpu.make_async_copy(src, wx.at[k, z, r], r_w.at[k, z])
        return mine, away, here

    for k in range(2):
        for h in range(2):
            for r in range(2):
                mine, away, here = weight_send(k, h, r)
                pl.when(jnp.logical_not(mine))(away.start)
                pl.when(mine)(here.start)

    info_arrived(0, lambda d: info.at[c, y, x, lax.rem(z + 4 - d, 4)])
    for d in range(1, 4):
        info_send(1, info.at[c, y, x], d, place(x + d, c, y, z)).start()
    for j in (1, 3, 2):
        forward(j)
    relay(0)

    def fill_left(k, salt):
        def body(i, _):
            term = (sub + (fsdp * width + i * 32)) * COLUMN_STEP + salt * SALT_STEP
            at = pl.ds(pl.multiple_of(i * 32, 32), 32)
            for r in range(16):
                lt[k, at, r * 128 : (r + 1) * 128] = levels_of(
                    seed_mul[r : r + 1, :] + term
                ).astype(jnp.bfloat16)
            return 0

        lax.fori_loop(0, width // 32, body, 0)

    fill_left(0, 1)
    info_arrived(1, lambda d: info.at[c, y, lax.rem(x + 4 - d, 4)])
    for d in range(1, 4):
        info_send(2, info.at[c, y], d, place(x, c, y + d, z)).start()
    relay(1)
    fill_left(1, 3)
    relay(3)
    info_arrived(2, lambda d: info.at[c, lax.rem(y + 4 - d, 4)])
    remote(info.at[c], info.at[c], s_ic, r_ic, partner).start()
    remote(info.at[1 - c], info.at[1 - c], s_ic, r_ic, partner).wait_recv()

    relay(2)

    lane = lax.broadcasted_iota(jnp.int32, (1, 128), 1) // 16
    for r in range(16):
        p, k = r // 2, r % 2
        row = jnp.zeros((1, 128), jnp.float32)
        for s in range(8):
            tile = info[p % 2, 2 * k + s // 4, p // 2, s % 4, 0:1, :]
            row = jnp.where(lane == s, tile, row)
        scaled[r : r + 1, :] = row
    whole = scaled[...]
    center = jnp.sum(jnp.sum(whole, axis=1, keepdims=True), axis=0, keepdims=True) / MEMBERS
    apart = whole - center
    spread = (
        jnp.sum(jnp.sum(apart * apart, axis=1, keepdims=True), axis=0, keepdims=True) / MEMBERS
    )
    scaled[...] = apart / jnp.sqrt(spread + stat_epsilon)

    chunk = wt.shape[0]

    def gradient(k, salt, first, last):
        def body(i, _):
            def fill(q, _):
                term = (sub + (pop * units + i * chunk + q * 32)) * COLUMN_STEP + salt * SALT_STEP
                at = pl.ds(pl.multiple_of(q * 32, 32), 32)
                for r in range(16):
                    wt[at, r * 128 : (r + 1) * 128] = (
                        levels_of(seed_mul[r : r + 1, :] + term) * scaled[r : r + 1, :]
                    ).astype(jnp.bfloat16)
                return 0

            lax.fori_loop(0, chunk // 32, fill, 0)
            total = lax.dot_general(
                lt[k], wt[...], (((1,), (1,)), ((), ())), preferred_element_type=jnp.float32
            )
            gb[k, :, pl.ds(pl.multiple_of(i * chunk, chunk), chunk)] = total * (
                1.0 / (MEMBERS * noise_scale) / 16384.0
            )
            return 0

        lax.fori_loop(first, last, body, 0)

    chunks = units // chunk

    def weights_arrive(k):
        for s in range(4):
            mine = wx.at[k, s, c]
            remote(mine, mine, s_w.at[k, 0], r_w.at[k, s], partner).wait_recv()
            remote(mine, mine, s_c.at[k, s], r_c.at[k, s], partner).start()
        for s in range(4):
            other = wx.at[k, s, 1 - c]
            remote(other, other, s_c.at[k, s], r_c.at[k, s], partner).wait_recv()

    def rows_arrive():
        for j in range(4):
            for way in range(2):
                half_over_x(x + 2, way, j).wait_recv()
        for s in range(4):
            xk[s] = xg[s].reshape(4 * width, 256).T

    def product(k, d):
        return jnp.dot(
            xk[lax.rem(y + d, 4)],
            wx[k].reshape(4 * width, half),
            preferred_element_type=jnp.float32,
        )

    def code(k, b, codes, scales):
        at = slice(b * 128, (b + 1) * 128)
        top = jnp.max(jnp.abs(p0[0, k, at]), axis=1, keepdims=True)
        top = jnp.maximum(top, 1e-30)
        grown = p0[0, k, at] * (LEVELS / top)
        whole_number = (grown + ROUNDER) - ROUNDER
        codes[...] = whole_number.astype(jnp.int32).astype(jnp.int16)
        scales[...] = row_of(top * (1.0 / LEVELS), eye)

    def far_send(k, way):
        there = place(x, c, y + 1 + 2 * way, z)
        return (
            remote(fs.at[k, way], fr.at[k, way], s_f.at[k, way], r_f.at[k, way], there),
            remote(fq.at[k, way], fp.at[k, way], s_g.at[k, way], r_g.at[k, way], there),
        )

    def near_send(k, way):
        there = place(x, c, y + 1 + 2 * way, z)
        return (
            remote(ps.at[k, way], pr.at[k, way], s_p.at[k, way], r_p.at[k, way], there),
            remote(sc.at[k, way], sr.at[k, way], s_q.at[k, way], r_q.at[k, way], there),
        )

    def far(k):
        p0[0, k] = product(k, 2)
        for way in range(2):
            code(k, way, fs.at[k, way], fq.at[k, way, 0:1])
            for part in far_send(k, way):
                part.start()

    def near(k, way):
        p0[0, k] = product(k, 1 + 2 * way)
        for part in far_send(k, way):
            part.wait_recv()
        at = slice(way * 128, (way + 1) * 128)
        step = column_of(fp[k, way, 0:1, :], eye)
        p0[0, k, at] = p0[0, k, at] + fr[k, way].astype(jnp.int32).astype(jnp.float32) * step
        for b in range(2):
            code(k, b, ps.at[k, way, b * 128 : (b + 1) * 128], sc.at[k, way, b : b + 1])
        for part in near_send(k, way):
            part.start()

    gradient(0, 2, 0, EARLY)
    weights_arrive(0)
    rows_arrive()
    far(0)
    weights_arrive(1)
    far(1)
    p0[1, 0] = product(0, 0)
    p0[1, 1] = product(1, 0)
    for k in range(2):
        for way in range(2):
            near(k, way)

    gradient(0, 2, EARLY, chunks)
    copy_gate = pltpu.make_async_copy(gb.at[0], grad_gate, l_g.at[0])
    copy_gate.start()
    gradient(1, 4, 0, chunks)
    copy_up = pltpu.make_async_copy(gb.at[1], grad_up, l_g.at[1])
    copy_up.start()

    for k in range(2):
        for way in range(2):
            for part in near_send(k, way):
                part.wait_recv()

    first_unit = (2 * x + z_core) * units + z_half * half
    for b in range(2):
        at = slice(b * 128, (b + 1) * 128)
        seed_row = seeds[pl.ds(2 * (2 * y + c) + b, 1), :].astype(jnp.float32)
        seed_col = column_of(seed_row, eye).astype(jnp.int32) * SEED_STEP
        along = []
        for k in range(2):
            row = jnp.zeros((1, 128), jnp.float32)
            for yy in range(4):
                for zz in range(4):
                    row = row + info[c, yy, y, zz, 1 + 2 * k + b : 2 + 2 * k + b, :]
            along.append(column_of(row, eye) * noise_scale)
        steps = [[column_of(sr[k, d, b : b + 1, :], eye) for d in range(2)] for k in range(2)]

        def finish(j, _):
            out = []
            for k, salt in ((0, 2), (1, 4)):
                over = pl.ds(pl.multiple_of(j * 128, 128), 128)
                total = p0[1, k, at, over]
                for d in range(2):
                    total = total + pr[k, d, at, over].astype(jnp.int32).astype(
                        jnp.float32
                    ) * steps[k][d]
                columns = (
                    lax.broadcasted_iota(jnp.int32, (1, 128), 1) + (first_unit + j * 128)
                ) * COLUMN_STEP + salt * SALT_STEP
                right = levels_of(seed_col + columns) * (1.0 / 128.0)
                out.append(total + along[k] * right)
            gate, up = out
            value = gate / (1.0 + jnp.exp(-gate)) * up
            hs[b, :, pl.ds(pl.multiple_of(j * 128, 128), 128)] = value.astype(jnp.bfloat16)
            return 0

        lax.fori_loop(0, half // 128, finish, 0)
        mine = jnp.logical_and(z_core == c, 2 * c + b == z)
        away = remote(
            hs.at[b], ho.at[z_half], s_h.at[b], r_h.at[z_half], place(x, z_core, y, 2 * c + b)
        )
        here = pltpu.make_async_copy(hs.at[b], ho.at[z_half], r_h.at[z_half])
        pl.when(jnp.logical_not(mine))(away.start)
        pl.when(mine)(here.start)

    for h in range(2):
        remote(ho.at[h], ho.at[h], s_h.at[0], r_h.at[h], partner).wait_recv()
        hidden[:, h * half : (h + 1) * half] = ho[h]

    for d in range(1, 4):
        remote(tokens, xg.at[x, z], s_xz.at[d - 1], r_xz.at[d - 1], partner).wait_send()
        info_send(0, info.at[c, y, x, z], d, partner).wait_send()
        info_send(1, info.at[c, y, x], d, partner).wait_send()
        info_send(2, info.at[c, y], d, partner).wait_send()
    for way in range(2):
        for j in range(4):
            over_x(piece_of(x, j), way, j).wait_send()
            half_over_x(x + 2, way, j).wait_send()
        for k in range(2):
            for part in far_send(k, way) + near_send(k, way):
                part.wait_send()
    remote(info.at[c], info.at[c], s_ic, r_ic, partner).wait_send()
    for k in range(2):
        for h in range(2):
            for r in range(2):
                mine, away, here = weight_send(k, h, r)
                pl.when(jnp.logical_not(mine))(away.wait_send)
        for s in range(4):
            mine = wx.at[k, s, c]
            remote(mine, mine, s_c.at[k, s], r_c.at[k, s], partner).wait_send()
    for b in range(2):
        mine = jnp.logical_and(z_core == c, 2 * c + b == z)
        away = remote(
            hs.at[b], ho.at[z_half], s_h.at[b], r_h.at[z_half], place(x, z_core, y, 2 * c + b)
        )
        pl.when(jnp.logical_not(mine))(away.wait_send)
    copy_gate.wait()
    copy_up.wait()


def adam_step(weight, first, second, grad):
    first_new = beta_first * first + (1.0 - beta_first) * grad
    second_new = beta_second * second + (1.0 - beta_second) * grad * grad
    moved = weight.astype(jnp.float32) + learn_rate * first_new / (
        jnp.sqrt(second_new) + adam_floor
    )
    return (moved.astype(jnp.bfloat16), first_new, second_new)


def shards(
    tokens, seeds, fitness, gate_weight, up_weight, gate_first, up_first, gate_second, up_second
):
    width, units = gate_weight.shape
    half = units // 2
    rows = tokens.shape[0]
    tokens = tokens.T
    bf, f32, i32, i16 = jnp.bfloat16, jnp.float32, jnp.int32, jnp.int16
    vmem = pl.BlockSpec(memory_space=pltpu.VMEM)
    anywhere = pl.BlockSpec(memory_space=pl.ANY)
    dma = pltpu.SemaphoreType.DMA
    tile = jnp.broadcast_to(jnp.tile(fitness, 8)[None], (8, 128))
    hidden, grad_gate, grad_up = pl.pallas_call(
        kernel,
        name="generation",
        out_shape=(
            jax.ShapeDtypeStruct((rows // 2, units), bf),
            jax.ShapeDtypeStruct((width, units), f32),
            jax.ShapeDtypeStruct((width, units), f32),
        ),
        in_specs=[anywhere, vmem, vmem, anywhere, anywhere],
        out_specs=(vmem, anywhere, anywhere),
        scratch_shapes=[
            pltpu.VMEM((4, 4, width, rows), bf),
            pltpu.VMEM((4, rows, 4 * width), bf),
            pltpu.VMEM((2, 4, 2, width // 2, half), bf),
            pltpu.VMEM((2, 4, 4, 4, 8, 128), f32),
            pltpu.VMEM((16, 128), i32),
            pltpu.VMEM((16, 128), f32),
            pltpu.VMEM((2, 2, rows, half), i16),
            pltpu.VMEM((2, 2, 8, 128), f32),
            pltpu.VMEM((2, 2, rows, half), i16),
            pltpu.VMEM((2, 2, 8, 128), f32),
            pltpu.VMEM((2, 2, rows // 2, half), i16),
            pltpu.VMEM((2, 2, 8, 128), f32),
            pltpu.VMEM((2, 2, rows // 2, half), i16),
            pltpu.VMEM((2, 2, 8, 128), f32),
            pltpu.VMEM((2, 2, rows, half), f32),
            pltpu.VMEM((2, width, MEMBERS), bf),
            pltpu.VMEM((256, MEMBERS), bf),
            pltpu.VMEM((2, width, units), f32),
            pltpu.VMEM((2, rows // 2, half), bf),
            pltpu.VMEM((2, rows // 2, half), bf),
            dma((3,)),
            dma((3,)),
            dma((2, 4)),
            dma((2, 4)),
            dma((2, 4)),
            dma((2, 4)),
            dma,
            dma((2, 4)),
            dma((2, 4)),
            dma((2, 4)),
            dma((2, 4)),
            dma((3, 3)),
            dma((3, 3)),
            dma,
            dma,
            dma((2, 2)),
            dma((2, 2)),
            dma((2, 2)),
            dma((2, 2)),
            dma((2, 2)),
            dma((2, 2)),
            dma((2, 2)),
            dma((2, 2)),
            dma((2,)),
            dma((2,)),
            dma((2,)),
        ],
        compiler_params=pltpu.CompilerParams(
            collective_id=0, has_side_effects=True, vmem_limit_bytes=56 << 20
        ),
    )(tokens, seeds.reshape(16, 128), tile, gate_weight, up_weight)
    gate_new, gate_first_new, gate_second_new = adam_step(
        gate_weight, gate_first, gate_second, grad_gate
    )
    up_new, up_first_new, up_second_new = adam_step(up_weight, up_first, up_second, grad_up)
    return (hidden, gate_new, up_new, gate_first_new, up_first_new, gate_second_new, up_second_new)


def solution(mesh):
    spread = P("fsdp", "pop")
    return jax.shard_map(
        shards,
        mesh=mesh,
        in_specs=(P("pop", "fsdp"), P(), P(("pop", "fsdp"))) + (spread,) * 6,
        out_specs=(spread,) * 7,
        check_vma=False,
    )
```

```python
import functools

import jax
import jax.numpy as jnp
from jax import lax
from jax.experimental import pallas as pl
from jax.experimental.pallas import tpu as pltpu
from jax.sharding import PartitionSpec as P

MESH = pl.DeviceIdType.MESH

noise_scale = 0.01
learn_rate = 0.002
beta_first = 0.9
beta_second = 0.99
adam_floor = 1e-08
stat_epsilon = 1e-06

MEMBERS = 2048
SEED_STEP = 1103515245
COLUMN_STEP = 40503
SALT_STEP = 7919
MIX = 73244475
LEVELS = 32767.0
EARLY = 3
ROUNDER = 12582912.0


def levels_of(mixed):
    mixed = mixed ^ (mixed >> 15)
    mixed = mixed * MIX
    mixed = mixed ^ (mixed >> 13)
    return (mixed & 255).astype(jnp.float32) - 127.5


def column_of(row, eye):
    return jnp.sum(jnp.where(eye, row, 0.0), axis=1, keepdims=True)


def row_of(column, eye):
    return jnp.sum(jnp.where(eye, column, 0.0), axis=0, keepdims=True)


def remote(src, dst, send_sem, recv_sem, device):
    return pltpu.make_async_remote_copy(
        src_ref=src,
        dst_ref=dst,
        send_sem=send_sem,
        recv_sem=recv_sem,
        device_id=device,
        device_id_type=MESH,
    )


def place(x, c, y, z):
    return {"pop": 2 * lax.rem(x, 4) + c, "fsdp": 4 * lax.rem(y, 4) + lax.rem(z, 4)}


def kernel(
    tokens,
    seeds,
    fitness,
    gate_w,
    up_w,
    hidden,
    grad_gate,
    grad_up,
    xg,
    xk,
    wx,
    info,
    seed_mul,
    scaled,
    ps,
    sc,
    pr,
    sr,
    fs,
    fq,
    fr,
    fp,
    p0,
    lt,
    wt,
    gb,
    hs,
    ho,
    s_xz,
    r_xz,
    s_xx,
    r_xx,
    s_xr,
    r_xr,
    l_x,
    s_w,
    r_w,
    s_c,
    r_c,
    s_i,
    r_i,
    s_ic,
    r_ic,
    s_p,
    r_p,
    s_q,
    r_q,
    s_f,
    r_f,
    s_g,
    r_g,
    s_h,
    r_h,
    l_g,
):
    pop = lax.axis_index("pop")
    fsdp = lax.axis_index("fsdp")
    x, c = pop // 2, pop % 2
    y, z = fsdp // 4, fsdp % 4
    width = tokens.shape[0]
    half = wx.shape[4]
    units = 2 * half
    z_core, z_half = z // 2, z % 2
    split = width // 2
    partner = place(x, 1 - c, y, z)

    barrier = pltpu.get_barrier_semaphore()
    for dc in range(2):
        for dz in range(4):
            if dc or dz:
                pl.semaphore_signal(
                    barrier,
                    inc=1,
                    device_id=place(x, (c + dc) % 2, y, z + dz),
                    device_id_type=MESH,
                )
    for d in range(1, 4):
        pl.semaphore_signal(barrier, inc=1, device_id=place(x + d, c, y, z), device_id_type=MESH)
        pl.semaphore_signal(barrier, inc=1, device_id=place(x, c, y + d, z), device_id_type=MESH)
    pl.semaphore_wait(barrier, 13)

    for d in (1, 3, 2):
        remote(tokens, xg.at[x, z], s_xz.at[d - 1], r_xz.at[d - 1], place(x, c, y, z + d)).start()
    for way in range(2):
        remote(
            tokens,
            xg.at[x, z],
            s_xx.at[way, 0],
            r_xx.at[way, 0],
            place(x + 1 + 2 * way, c, y, z),
        ).start()
    own = pltpu.make_async_copy(tokens, xg.at[x, z], l_x)
    own.start()

    eye = lax.broadcasted_iota(jnp.int32, (128, 128), 0) == lax.broadcasted_iota(
        jnp.int32, (128, 128), 1
    )
    seed_mul[...] = seeds[...] * SEED_STEP
    my_info = info.at[c, y, x, z]
    my_info[...] = jnp.zeros((8, 128), jnp.float32)
    my_info[0:1, 0:16] = fitness[...]
    my_info[...] = pltpu.roll(my_info[...], 16 * lax.rem(fsdp, 8), 1)
    sub = lax.broadcasted_iota(jnp.int32, (32, 128), 0)
    own.wait()
    for b in range(2):
        seed_row = seeds[pl.ds(2 * pop + b, 1), :] * SEED_STEP

        def add_along(i, sums):
            at = pl.ds(pl.multiple_of(i * 32, 32), 32)
            rows = xg[x, z, at, b * 128 : (b + 1) * 128].astype(jnp.float32)
            term = (sub + (fsdp * width + i * 32)) * COLUMN_STEP
            return tuple(
                kept + rows * levels_of(seed_row + (term + salt * SALT_STEP))
                for kept, salt in zip(sums, (1, 3))
            )

        zero = jnp.zeros((32, 128), jnp.float32)
        sums = lax.fori_loop(0, width // 32, add_along, (zero, zero))
        for k in range(2):
            my_info[1 + 2 * k + b : 2 + 2 * k + b, :] = jnp.sum(
                sums[k], axis=0, keepdims=True
            ) * (1.0 / 128.0)

    def info_send(stage, ref, d, device):
        return remote(ref, ref, s_i.at[stage, d - 1], r_i.at[stage, d - 1], device)

    for d in range(1, 4):
        info_send(0, info.at[c, y, x, z], d, place(x, c, y, z + d)).start()

    def piece_of(source, j):
        return xg.at[lax.rem(source, 4), lax.rem(z + 4 - j, 4)]

    def over_x(piece, way, j):
        there = place(x + 1 + 2 * way, c, y, z)
        return remote(piece, piece, s_xx.at[way, j], r_xx.at[way, j], there)

    def half_over_x(source, way, j):
        piece = piece_of(source, j).at[way * split : (way + 1) * split]
        there = place(x + 1 + 2 * way, c, y, z)
        return remote(piece, piece, s_xr.at[way, j], r_xr.at[way, j], there)

    def forward(j):
        piece = piece_of(x, j)
        remote(piece, piece, s_xz.at[j - 1], r_xz.at[j - 1], place(x, c, y, z + j)).wait_recv()
        for way in range(2):
            over_x(piece, way, j).start()

    def relay(j):
        for way in range(2):
            source = x + 3 - 2 * way
            over_x(piece_of(source, j), way, j).wait_recv()
            half_over_x(source, way, j).start()

    def info_arrived(stage, ref_of):
        for d in range(1, 4):
            info_send(stage, ref_of(d), d, partner).wait_recv()

    def weight_send(k, h, r):
        src = (gate_w, up_w)[k].at[r * split : (r + 1) * split, h * half : (h + 1) * half]
        mine = jnp.logical_and(c == r, 2 * c + h == z)
        away = remote(
            src, wx.at[k, z, r], s_w.at[k, 2 * h + r], r_w.at[k, z], place(x, r, y, 2 * c + h)
        )
        here = pltpu.make_async_copy(src, wx.at[k, z, r], r_w.at[k, z])
        return mine, away, here

    for k in range(2):
        for h in range(2):
            for r in range(2):
                mine, away, here = weight_send(k, h, r)
                pl.when(jnp.logical_not(mine))(away.start)
                pl.when(mine)(here.start)

    forward(1)
    forward(3)
    relay(0)
    info_arrived(0, lambda d: info.at[c, y, x, lax.rem(z + 4 - d, 4)])
    for d in range(1, 4):
        info_send(1, info.at[c, y, x], d, place(x + d, c, y, z)).start()
    forward(2)

    def fill_left(k, salt):
        def body(i, _):
            term = (sub + (fsdp * width + i * 32)) * COLUMN_STEP + salt * SALT_STEP
            at = pl.ds(pl.multiple_of(i * 32, 32), 32)
            for r in range(16):
                lt[k, at, r * 128 : (r + 1) * 128] = levels_of(
                    seed_mul[r : r + 1, :] + term
                ).astype(jnp.bfloat16)
            return 0

        lax.fori_loop(0, width // 32, body, 0)

    fill_left(0, 1)
    relay(1)
    relay(3)
    info_arrived(1, lambda d: info.at[c, y, lax.rem(x + 4 - d, 4)])
    for d in range(1, 4):
        info_send(2, info.at[c, y], d, place(x, c, y + d, z)).start()
    fill_left(1, 3)
    info_arrived(2, lambda d: info.at[c, lax.rem(y + 4 - d, 4)])
    remote(info.at[c], info.at[c], s_ic, r_ic, partner).start()
    relay(2)
    remote(info.at[1 - c], info.at[1 - c], s_ic, r_ic, partner).wait_recv()

    lane = lax.broadcasted_iota(jnp.int32, (1, 128), 1) // 16
    for r in range(16):
        p, k = r // 2, r % 2
        row = jnp.zeros((1, 128), jnp.float32)
        for s in range(8):
            tile = info[p % 2, 2 * k + s // 4, p // 2, s % 4, 0:1, :]
            row = jnp.where(lane == s, tile, row)
        scaled[r : r + 1, :] = row
    whole = scaled[...]
    center = jnp.sum(jnp.sum(whole, axis=1, keepdims=True), axis=0, keepdims=True) / MEMBERS
    apart = whole - center
    spread = (
        jnp.sum(jnp.sum(apart * apart, axis=1, keepdims=True), axis=0, keepdims=True) / MEMBERS
    )
    scaled[...] = apart / jnp.sqrt(spread + stat_epsilon)

    chunk = wt.shape[0]

    def gradient(k, salt, first, last):
        def body(i, _):
            def fill(q, _):
                term = (sub + (pop * units + i * chunk + q * 32)) * COLUMN_STEP + salt * SALT_STEP
                at = pl.ds(pl.multiple_of(q * 32, 32), 32)
                for r in range(16):
                    wt[at, r * 128 : (r + 1) * 128] = (
                        levels_of(seed_mul[r : r + 1, :] + term) * scaled[r : r + 1, :]
                    ).astype(jnp.bfloat16)
                return 0

            lax.fori_loop(0, chunk // 32, fill, 0)
            total = lax.dot_general(
                lt[k], wt[...], (((1,), (1,)), ((), ())), preferred_element_type=jnp.float32
            )
            gb[k, :, pl.ds(pl.multiple_of(i * chunk, chunk), chunk)] = total * (
                1.0 / (MEMBERS * noise_scale) / 16384.0
            )
            return 0

        lax.fori_loop(first, last, body, 0)

    chunks = units // chunk

    def weights_share(k):
        for s in range(4):
            mine = wx.at[k, s, c]
            remote(mine, mine, s_w.at[k, 0], r_w.at[k, s], partner).wait_recv()
            remote(mine, mine, s_c.at[k, s], r_c.at[k, s], partner).start()

    def weights_arrive(k):
        for s in range(4):
            other = wx.at[k, s, 1 - c]
            remote(other, other, s_c.at[k, s], r_c.at[k, s], partner).wait_recv()

    def rows_arrive():
        for j in range(4):
            for way in range(2):
                half_over_x(x + 2, way, j).wait_recv()

    def turn(d):
        xk[d] = xg[lax.rem(y + d, 4)].reshape(4 * width, 256).T

    def product(k, d):
        return jnp.dot(
            xk[d],
            wx[k].reshape(4 * width, half),
            preferred_element_type=jnp.float32,
        )

    def code(k, b, codes, scales):
        at = slice(b * 128, (b + 1) * 128)
        top = jnp.max(jnp.abs(p0[0, k, at]), axis=1, keepdims=True)
        top = jnp.maximum(top, 1e-30)
        grown = p0[0, k, at] * (LEVELS / top)
        whole_number = (grown + ROUNDER) - ROUNDER
        codes[...] = whole_number.astype(jnp.int32).astype(jnp.int16)
        scales[...] = row_of(top * (1.0 / LEVELS), eye)

    def far_send(k, way):
        there = place(x, c, y + 1 + 2 * way, z)
        return (
            remote(fs.at[k, way], fr.at[k, way], s_f.at[k, way], r_f.at[k, way], there),
            remote(fq.at[k, way], fp.at[k, way], s_g.at[k, way], r_g.at[k, way], there),
        )

    def near_send(k, way, b):
        there = place(x, c, y + 1 + 2 * way, z)
        return (
            remote(
                ps.at[k, way, b], pr.at[k, way, b], s_p.at[k, way, b], r_p.at[k, way, b], there
            ),
            remote(
                sc.at[k, way, b], sr.at[k, way, b], s_q.at[k, way, b], r_q.at[k, way, b], there
            ),
        )

    def far(k):
        p0[0, k] = product(k, 2)
        for way in range(2):
            code(k, way, fs.at[k, way], fq.at[k, way, 0:1])
            for part in far_send(k, way):
                part.start()

    def near(k, way):
        p0[0, k] = product(k, 1 + 2 * way)
        for part in far_send(k, way):
            part.wait_recv()
        at = slice(way * 128, (way + 1) * 128)
        step = column_of(fp[k, way, 0:1, :], eye)
        p0[0, k, at] = p0[0, k, at] + fr[k, way].astype(jnp.int32).astype(jnp.float32) * step
        for b in range(2):
            code(k, b, ps.at[k, way, b], sc.at[k, way, b, 0:1])
            for part in near_send(k, way, b):
                part.start()

    gradient(0, 2, 0, EARLY)
    weights_share(0)
    rows_arrive()
    turn(2)
    weights_arrive(0)
    far(0)
    weights_share(1)
    turn(0)
    p0[1, 0] = product(0, 0)
    weights_arrive(1)
    far(1)
    turn(1)
    near(0, 0)
    turn(3)
    near(0, 1)
    p0[1, 1] = product(1, 0)
    near(1, 0)
    near(1, 1)

    gradient(0, 2, EARLY, chunks)
    copy_gate = pltpu.make_async_copy(gb.at[0], grad_gate, l_g.at[0])
    copy_gate.start()
    gradient(1, 4, 0, chunks)
    copy_up = pltpu.make_async_copy(gb.at[1], grad_up, l_g.at[1])
    copy_up.start()

    first_unit = (2 * x + z_core) * units + z_half * half
    for b in range(2):
        for k in range(2):
            for way in range(2):
                for part in near_send(k, way, b):
                    part.wait_recv()
        at = slice(b * 128, (b + 1) * 128)
        seed_row = seeds[pl.ds(2 * (2 * y + c) + b, 1), :].astype(jnp.float32)
        seed_col = column_of(seed_row, eye).astype(jnp.int32) * SEED_STEP
        along = []
        for k in range(2):
            row = jnp.zeros((1, 128), jnp.float32)
            for yy in range(4):
                for zz in range(4):
                    row = row + info[c, yy, y, zz, 1 + 2 * k + b : 2 + 2 * k + b, :]
            along.append(column_of(row, eye) * noise_scale)
        steps = [[column_of(sr[k, d, b, 0:1, :], eye) for d in range(2)] for k in range(2)]

        def finish(j, _):
            out = []
            for k, salt in ((0, 2), (1, 4)):
                over = pl.ds(pl.multiple_of(j * 128, 128), 128)
                total = p0[1, k, at, over]
                for d in range(2):
                    total = total + pr[k, d, b, :, over].astype(jnp.int32).astype(
                        jnp.float32
                    ) * steps[k][d]
                columns = (
                    lax.broadcasted_iota(jnp.int32, (1, 128), 1) + (first_unit + j * 128)
                ) * COLUMN_STEP + salt * SALT_STEP
                right = levels_of(seed_col + columns) * (1.0 / 128.0)
                out.append(total + along[k] * right)
            gate, up = out
            value = gate / (1.0 + jnp.exp(-gate)) * up
            hs[b, :, pl.ds(pl.multiple_of(j * 128, 128), 128)] = value.astype(jnp.bfloat16)
            return 0

        lax.fori_loop(0, half // 128, finish, 0)
        mine = jnp.logical_and(z_core == c, 2 * c + b == z)
        away = remote(
            hs.at[b], ho.at[z_half], s_h.at[b], r_h.at[z_half], place(x, z_core, y, 2 * c + b)
        )
        here = pltpu.make_async_copy(hs.at[b], ho.at[z_half], r_h.at[z_half])
        pl.when(jnp.logical_not(mine))(away.start)
        pl.when(mine)(here.start)

    for h in range(2):
        remote(ho.at[h], ho.at[h], s_h.at[0], r_h.at[h], partner).wait_recv()
        hidden[:, h * half : (h + 1) * half] = ho[h]

    for d in range(1, 4):
        remote(tokens, xg.at[x, z], s_xz.at[d - 1], r_xz.at[d - 1], partner).wait_send()
        info_send(0, info.at[c, y, x, z], d, partner).wait_send()
        info_send(1, info.at[c, y, x], d, partner).wait_send()
        info_send(2, info.at[c, y], d, partner).wait_send()
    for way in range(2):
        for j in range(4):
            over_x(piece_of(x, j), way, j).wait_send()
            half_over_x(x + 2, way, j).wait_send()
        for k in range(2):
            for part in far_send(k, way) + near_send(k, way, 0) + near_send(k, way, 1):
                part.wait_send()
    remote(info.at[c], info.at[c], s_ic, r_ic, partner).wait_send()
    for k in range(2):
        for h in range(2):
            for r in range(2):
                mine, away, here = weight_send(k, h, r)
                pl.when(jnp.logical_not(mine))(away.wait_send)
        for s in range(4):
            mine = wx.at[k, s, c]
            remote(mine, mine, s_c.at[k, s], r_c.at[k, s], partner).wait_send()
    for b in range(2):
        mine = jnp.logical_and(z_core == c, 2 * c + b == z)
        away = remote(
            hs.at[b], ho.at[z_half], s_h.at[b], r_h.at[z_half], place(x, z_core, y, 2 * c + b)
        )
        pl.when(jnp.logical_not(mine))(away.wait_send)
    copy_gate.wait()
    copy_up.wait()


def adam_step(weight, first, second, grad):
    first_new = beta_first * first + (1.0 - beta_first) * grad
    second_new = beta_second * second + (1.0 - beta_second) * grad * grad
    moved = weight.astype(jnp.float32) + learn_rate * first_new / (
        jnp.sqrt(second_new) + adam_floor
    )
    return (moved.astype(jnp.bfloat16), first_new, second_new)


def shards(
    tokens, seeds, fitness, gate_weight, up_weight, gate_first, up_first, gate_second, up_second
):
    width, units = gate_weight.shape
    half = units // 2
    rows = tokens.shape[0]
    tokens = tokens.T
    bf, f32, i32, i16 = jnp.bfloat16, jnp.float32, jnp.int32, jnp.int16
    vmem = pl.BlockSpec(memory_space=pltpu.VMEM)
    anywhere = pl.BlockSpec(memory_space=pl.ANY)
    dma = pltpu.SemaphoreType.DMA
    hidden, grad_gate, grad_up = pl.pallas_call(
        kernel,
        name="generation",
        out_shape=(
            jax.ShapeDtypeStruct((rows // 2, units), bf),
            jax.ShapeDtypeStruct((width, units), f32),
            jax.ShapeDtypeStruct((width, units), f32),
        ),
        in_specs=[anywhere, vmem, vmem, anywhere, anywhere],
        out_specs=(vmem, anywhere, anywhere),
        scratch_shapes=[
            pltpu.VMEM((4, 4, width, rows), bf),
            pltpu.VMEM((4, rows, 4 * width), bf),
            pltpu.VMEM((2, 4, 2, width // 2, half), bf),
            pltpu.VMEM((2, 4, 4, 4, 8, 128), f32),
            pltpu.VMEM((16, 128), i32),
            pltpu.VMEM((16, 128), f32),
            pltpu.VMEM((2, 2, 2, rows // 2, half), i16),
            pltpu.VMEM((2, 2, 2, 8, 128), f32),
            pltpu.VMEM((2, 2, 2, rows // 2, half), i16),
            pltpu.VMEM((2, 2, 2, 8, 128), f32),
            pltpu.VMEM((2, 2, rows // 2, half), i16),
            pltpu.VMEM((2, 2, 8, 128), f32),
            pltpu.VMEM((2, 2, rows // 2, half), i16),
            pltpu.VMEM((2, 2, 8, 128), f32),
            pltpu.VMEM((2, 2, rows, half), f32),
            pltpu.VMEM((2, width, MEMBERS), bf),
            pltpu.VMEM((256, MEMBERS), bf),
            pltpu.VMEM((2, width, units), f32),
            pltpu.VMEM((2, rows // 2, half), bf),
            pltpu.VMEM((2, rows // 2, half), bf),
            dma((3,)),
            dma((3,)),
            dma((2, 4)),
            dma((2, 4)),
            dma((2, 4)),
            dma((2, 4)),
            dma,
            dma((2, 4)),
            dma((2, 4)),
            dma((2, 4)),
            dma((2, 4)),
            dma((3, 3)),
            dma((3, 3)),
            dma,
            dma,
            dma((2, 2, 2)),
            dma((2, 2, 2)),
            dma((2, 2, 2)),
            dma((2, 2, 2)),
            dma((2, 2)),
            dma((2, 2)),
            dma((2, 2)),
            dma((2, 2)),
            dma((2,)),
            dma((2,)),
            dma((2,)),
        ],
        compiler_params=pltpu.CompilerParams(
            collective_id=0, has_side_effects=True, vmem_limit_bytes=56 << 20
        ),
    )(tokens, seeds.reshape(16, 128), fitness.reshape(1, 16), gate_weight, up_weight)
    gate_new, gate_first_new, gate_second_new = adam_step(
        gate_weight, gate_first, gate_second, grad_gate
    )
    up_new, up_first_new, up_second_new = adam_step(up_weight, up_first, up_second, grad_up)
    return (hidden, gate_new, up_new, gate_first_new, up_first_new, gate_second_new, up_second_new)


def solution(mesh):
    spread = P("fsdp", "pop")
    return jax.shard_map(
        shards,
        mesh=mesh,
        in_specs=(P("pop", "fsdp"), P(), P(("pop", "fsdp"))) + (spread,) * 6,
        out_specs=(spread,) * 7,
        check_vma=False,
    )
```

```python
import functools

import jax
import jax.numpy as jnp
from jax import lax
from jax.experimental import pallas as pl
from jax.experimental.pallas import tpu as pltpu
from jax.sharding import PartitionSpec as P

MESH = pl.DeviceIdType.MESH

noise_scale = 0.01
learn_rate = 0.002
beta_first = 0.9
beta_second = 0.99
adam_floor = 1e-08
stat_epsilon = 1e-06

MEMBERS = 2048
SEED_STEP = 1103515245
COLUMN_STEP = 40503
SALT_STEP = 7919
MIX = 73244475
LEVELS = 32767.0
EARLY = 3
ROUNDER = 12582912.0


def levels_of(mixed):
    mixed = mixed ^ (mixed >> 15)
    mixed = mixed * MIX
    mixed = mixed ^ (mixed >> 13)
    return (mixed & 255).astype(jnp.float32) - 127.5


def column_of(row, eye):
    return jnp.sum(jnp.where(eye, row, 0.0), axis=1, keepdims=True)


def row_of(column, eye):
    return jnp.sum(jnp.where(eye, column, 0.0), axis=0, keepdims=True)


def remote(src, dst, send_sem, recv_sem, device):
    return pltpu.make_async_remote_copy(
        src_ref=src,
        dst_ref=dst,
        send_sem=send_sem,
        recv_sem=recv_sem,
        device_id=device,
        device_id_type=MESH,
    )


def place(x, c, y, z):
    return {"pop": 2 * lax.rem(x, 4) + c, "fsdp": 4 * lax.rem(y, 4) + lax.rem(z, 4)}


def kernel(
    tokens,
    seeds,
    fitness,
    gate_w,
    up_w,
    hidden,
    grad_gate,
    grad_up,
    xg,
    xk,
    wx,
    info,
    seed_mul,
    scaled,
    ps,
    sc,
    pr,
    sr,
    fs,
    fq,
    fr,
    fp,
    p0,
    lt,
    wt,
    gb,
    hs,
    ho,
    s_xz,
    r_xz,
    s_xx,
    r_xx,
    s_xr,
    r_xr,
    l_x,
    s_w,
    r_w,
    s_c,
    r_c,
    s_i,
    r_i,
    s_ic,
    r_ic,
    s_p,
    r_p,
    s_q,
    r_q,
    s_f,
    r_f,
    s_g,
    r_g,
    s_h,
    r_h,
    l_g,
):
    pop = lax.axis_index("pop")
    fsdp = lax.axis_index("fsdp")
    x, c = pop // 2, pop % 2
    y, z = fsdp // 4, fsdp % 4
    width = tokens.shape[0]
    half = wx.shape[4]
    units = 2 * half
    z_core, z_half = z // 2, z % 2
    split = width // 2
    partner = place(x, 1 - c, y, z)

    barrier = pltpu.get_barrier_semaphore()
    for dc in range(2):
        for dz in range(4):
            if dc or dz:
                pl.semaphore_signal(
                    barrier,
                    inc=1,
                    device_id=place(x, (c + dc) % 2, y, z + dz),
                    device_id_type=MESH,
                )
    for d in range(1, 4):
        pl.semaphore_signal(barrier, inc=1, device_id=place(x + d, c, y, z), device_id_type=MESH)
        pl.semaphore_signal(barrier, inc=1, device_id=place(x, c, y + d, z), device_id_type=MESH)
    pl.semaphore_wait(barrier, 13)

    for d in (1, 3, 2):
        remote(tokens, xg.at[x, z], s_xz.at[d - 1], r_xz.at[d - 1], place(x, c, y, z + d)).start()
    for way in range(2):
        remote(
            tokens,
            xg.at[x, z],
            s_xx.at[way, 0],
            r_xx.at[way, 0],
            place(x + 1 + 2 * way, c, y, z),
        ).start()
    own = pltpu.make_async_copy(tokens, xg.at[x, z], l_x)
    own.start()

    eye = lax.broadcasted_iota(jnp.int32, (128, 128), 0) == lax.broadcasted_iota(
        jnp.int32, (128, 128), 1
    )
    seed_mul[...] = seeds[...] * SEED_STEP
    my_info = info.at[c, y, x, z]
    my_info[...] = jnp.zeros((8, 128), jnp.float32)
    my_info[0:1, 0:16] = fitness[...]
    my_info[...] = pltpu.roll(my_info[...], 16 * lax.rem(fsdp, 8), 1)
    sub = lax.broadcasted_iota(jnp.int32, (32, 128), 0)
    own.wait()
    for b in range(2):
        seed_row = seeds[pl.ds(2 * pop + b, 1), :] * SEED_STEP

        def add_along(i, sums):
            at = pl.ds(pl.multiple_of(i * 32, 32), 32)
            rows = xg[x, z, at, b * 128 : (b + 1) * 128].astype(jnp.float32)
            term = (sub + (fsdp * width + i * 32)) * COLUMN_STEP
            return tuple(
                kept + rows * levels_of(seed_row + (term + salt * SALT_STEP))
                for kept, salt in zip(sums, (1, 3))
            )

        zero = jnp.zeros((32, 128), jnp.float32)
        sums = lax.fori_loop(0, width // 32, add_along, (zero, zero))
        for k in range(2):
            my_info[1 + 2 * k + b : 2 + 2 * k + b, :] = jnp.sum(
                sums[k], axis=0, keepdims=True
            ) * (1.0 / 128.0)

    def info_send(stage, ref, d, device):
        return remote(ref, ref, s_i.at[stage, d - 1], r_i.at[stage, d - 1], device)

    for d in range(1, 4):
        info_send(0, info.at[c, y, x, z], d, place(x, c, y, z + d)).start()

    def piece_of(source, j):
        return xg.at[lax.rem(source, 4), lax.rem(z + 4 - j, 4)]

    def over_x(piece, way, j):
        there = place(x + 1 + 2 * way, c, y, z)
        return remote(piece, piece, s_xx.at[way, j], r_xx.at[way, j], there)

    def half_over_x(source, way, j):
        piece = piece_of(source, j).at[way * split : (way + 1) * split]
        there = place(x + 1 + 2 * way, c, y, z)
        return remote(piece, piece, s_xr.at[way, j], r_xr.at[way, j], there)

    def forward(j):
        piece = piece_of(x, j)
        remote(piece, piece, s_xz.at[j - 1], r_xz.at[j - 1], place(x, c, y, z + j)).wait_recv()
        for way in range(2):
            over_x(piece, way, j).start()

    def relay(j):
        for way in range(2):
            source = x + 3 - 2 * way
            over_x(piece_of(source, j), way, j).wait_recv()
            half_over_x(source, way, j).start()

    def info_arrived(stage, ref_of):
        for d in range(1, 4):
            info_send(stage, ref_of(d), d, partner).wait_recv()

    def weight_send(k, h, r):
        src = (gate_w, up_w)[k].at[r * split : (r + 1) * split, h * half : (h + 1) * half]
        mine = jnp.logical_and(c == r, 2 * c + h == z)
        away = remote(
            src, wx.at[k, z, r], s_w.at[k, 2 * h + r], r_w.at[k, z], place(x, r, y, 2 * c + h)
        )
        here = pltpu.make_async_copy(src, wx.at[k, z, r], r_w.at[k, z])
        return mine, away, here

    for k in range(2):
        for h in range(2):
            for r in range(2):
                mine, away, here = weight_send(k, h, r)
                pl.when(jnp.logical_not(mine))(away.start)
                pl.when(mine)(here.start)

    forward(1)
    forward(3)
    relay(0)
    info_arrived(0, lambda d: info.at[c, y, x, lax.rem(z + 4 - d, 4)])
    for d in range(1, 4):
        info_send(1, info.at[c, y, x], d, place(x + d, c, y, z)).start()
    forward(2)

    def fill_left(k, salt):
        def body(i, _):
            term = (sub + (fsdp * width + i * 32)) * COLUMN_STEP + salt * SALT_STEP
            at = pl.ds(pl.multiple_of(i * 32, 32), 32)
            for r in range(16):
                lt[k, at, r * 128 : (r + 1) * 128] = levels_of(
                    seed_mul[r : r + 1, :] + term
                ).astype(jnp.bfloat16)
            return 0

        lax.fori_loop(0, width // 32, body, 0)

    fill_left(0, 1)
    relay(1)
    relay(3)
    info_arrived(1, lambda d: info.at[c, y, lax.rem(x + 4 - d, 4)])
    for d in range(1, 4):
        info_send(2, info.at[c, y], d, place(x, c, y + d, z)).start()
    fill_left(1, 3)
    info_arrived(2, lambda d: info.at[c, lax.rem(y + 4 - d, 4)])
    remote(info.at[c], info.at[c], s_ic, r_ic, partner).start()
    relay(2)
    remote(info.at[1 - c], info.at[1 - c], s_ic, r_ic, partner).wait_recv()

    lane = lax.broadcasted_iota(jnp.int32, (1, 128), 1) // 16
    for r in range(16):
        p, k = r // 2, r % 2
        row = jnp.zeros((1, 128), jnp.float32)
        for s in range(8):
            tile = info[p % 2, 2 * k + s // 4, p // 2, s % 4, 0:1, :]
            row = jnp.where(lane == s, tile, row)
        scaled[r : r + 1, :] = row
    whole = scaled[...]
    center = jnp.sum(jnp.sum(whole, axis=1, keepdims=True), axis=0, keepdims=True) / MEMBERS
    apart = whole - center
    spread = (
        jnp.sum(jnp.sum(apart * apart, axis=1, keepdims=True), axis=0, keepdims=True) / MEMBERS
    )
    scaled[...] = apart / jnp.sqrt(spread + stat_epsilon)

    chunk = wt.shape[0]

    def gradient(k, salt, first, last):
        def body(i, _):
            def fill(q, _):
                term = (sub + (pop * units + i * chunk + q * 32)) * COLUMN_STEP + salt * SALT_STEP
                at = pl.ds(pl.multiple_of(q * 32, 32), 32)
                for r in range(16):
                    wt[at, r * 128 : (r + 1) * 128] = (
                        levels_of(seed_mul[r : r + 1, :] + term) * scaled[r : r + 1, :]
                    ).astype(jnp.bfloat16)
                return 0

            lax.fori_loop(0, chunk // 32, fill, 0, unroll=2)
            total = lax.dot_general(
                lt[k], wt[...], (((1,), (1,)), ((), ())), preferred_element_type=jnp.float32
            )
            gb[k, :, pl.ds(pl.multiple_of(i * chunk, chunk), chunk)] = total * (
                1.0 / (MEMBERS * noise_scale) / 16384.0
            )
            return 0

        lax.fori_loop(first, last, body, 0)

    chunks = units // chunk

    def weights_share(k):
        for s in range(4):
            mine = wx.at[k, s, c]
            remote(mine, mine, s_w.at[k, 0], r_w.at[k, s], partner).wait_recv()
            remote(mine, mine, s_c.at[k, s], r_c.at[k, s], partner).start()

    def weights_arrive(k):
        for s in range(4):
            other = wx.at[k, s, 1 - c]
            remote(other, other, s_c.at[k, s], r_c.at[k, s], partner).wait_recv()

    def rows_arrive():
        for j in range(4):
            for way in range(2):
                half_over_x(x + 2, way, j).wait_recv()

    def turn(d):
        xk[d] = xg[lax.rem(y + d, 4)].reshape(4 * width, 256).T

    def product(k, d):
        return jnp.dot(
            xk[d],
            wx[k].reshape(4 * width, half),
            preferred_element_type=jnp.float32,
        )

    def code(k, b, codes, scales):
        at = slice(b * 128, (b + 1) * 128)
        top = jnp.max(jnp.abs(p0[0, k, at]), axis=1, keepdims=True)
        top = jnp.maximum(top, 1e-30)
        grown = p0[0, k, at] * (LEVELS / top)
        whole_number = (grown + ROUNDER) - ROUNDER
        codes[...] = whole_number.astype(jnp.int32).astype(jnp.int16)
        scales[...] = row_of(top * (1.0 / LEVELS), eye)

    def far_send(k, way):
        there = place(x, c, y + 1 + 2 * way, z)
        return (
            remote(fs.at[k, way], fr.at[k, way], s_f.at[k, way], r_f.at[k, way], there),
            remote(fq.at[k, way], fp.at[k, way], s_g.at[k, way], r_g.at[k, way], there),
        )

    def near_send(k, way, b):
        there = place(x, c, y + 1 + 2 * way, z)
        return (
            remote(
                ps.at[k, way, b], pr.at[k, way, b], s_p.at[k, way, b], r_p.at[k, way, b], there
            ),
            remote(
                sc.at[k, way, b], sr.at[k, way, b], s_q.at[k, way, b], r_q.at[k, way, b], there
            ),
        )

    def far(k):
        p0[0, k] = product(k, 2)
        for way in range(2):
            code(k, way, fs.at[k, way], fq.at[k, way, 0:1])
            for part in far_send(k, way):
                part.start()

    def near(k, way):
        p0[0, k] = product(k, 1 + 2 * way)
        for part in far_send(k, way):
            part.wait_recv()
        at = slice(way * 128, (way + 1) * 128)
        step = column_of(fp[k, way, 0:1, :], eye)
        p0[0, k, at] = p0[0, k, at] + fr[k, way].astype(jnp.int32).astype(jnp.float32) * step
        for b in range(2):
            code(k, b, ps.at[k, way, b], sc.at[k, way, b, 0:1])
            for part in near_send(k, way, b):
                part.start()

    gradient(0, 2, 0, EARLY)
    weights_share(0)
    rows_arrive()
    turn(2)
    weights_arrive(0)
    far(0)
    weights_share(1)
    turn(0)
    p0[1, 0] = product(0, 0)
    weights_arrive(1)
    far(1)
    turn(1)
    near(0, 0)
    turn(3)
    near(0, 1)
    p0[1, 1] = product(1, 0)
    near(1, 0)
    near(1, 1)

    gradient(0, 2, EARLY, chunks)
    copy_gate = pltpu.make_async_copy(gb.at[0], grad_gate, l_g.at[0])
    copy_gate.start()
    gradient(1, 4, 0, chunks)
    copy_up = pltpu.make_async_copy(gb.at[1], grad_up, l_g.at[1])
    copy_up.start()

    first_unit = (2 * x + z_core) * units + z_half * half
    for b in range(2):
        for k in range(2):
            for way in range(2):
                for part in near_send(k, way, b):
                    part.wait_recv()
        at = slice(b * 128, (b + 1) * 128)
        seed_row = seeds[pl.ds(2 * (2 * y + c) + b, 1), :].astype(jnp.float32)
        seed_col = column_of(seed_row, eye).astype(jnp.int32) * SEED_STEP
        along = []
        for k in range(2):
            row = jnp.zeros((1, 128), jnp.float32)
            for yy in range(4):
                for zz in range(4):
                    row = row + info[c, yy, y, zz, 1 + 2 * k + b : 2 + 2 * k + b, :]
            along.append(column_of(row, eye) * noise_scale)
        steps = [[column_of(sr[k, d, b, 0:1, :], eye) for d in range(2)] for k in range(2)]

        def finish(j, _):
            out = []
            for k, salt in ((0, 2), (1, 4)):
                over = pl.ds(pl.multiple_of(j * 128, 128), 128)
                total = p0[1, k, at, over]
                for d in range(2):
                    total = total + pr[k, d, b, :, over].astype(jnp.int32).astype(
                        jnp.float32
                    ) * steps[k][d]
                columns = (
                    lax.broadcasted_iota(jnp.int32, (1, 128), 1) + (first_unit + j * 128)
                ) * COLUMN_STEP + salt * SALT_STEP
                right = levels_of(seed_col + columns) * (1.0 / 128.0)
                out.append(total + along[k] * right)
            gate, up = out
            value = gate / (1.0 + jnp.exp(-gate)) * up
            hs[b, :, pl.ds(pl.multiple_of(j * 128, 128), 128)] = value.astype(jnp.bfloat16)
            return 0

        lax.fori_loop(0, half // 128, finish, 0)
        mine = jnp.logical_and(z_core == c, 2 * c + b == z)
        away = remote(
            hs.at[b], ho.at[z_half], s_h.at[b], r_h.at[z_half], place(x, z_core, y, 2 * c + b)
        )
        here = pltpu.make_async_copy(hs.at[b], ho.at[z_half], r_h.at[z_half])
        pl.when(jnp.logical_not(mine))(away.start)
        pl.when(mine)(here.start)

    for h in range(2):
        remote(ho.at[h], ho.at[h], s_h.at[0], r_h.at[h], partner).wait_recv()
        hidden[:, h * half : (h + 1) * half] = ho[h]

    for d in range(1, 4):
        remote(tokens, xg.at[x, z], s_xz.at[d - 1], r_xz.at[d - 1], partner).wait_send()
        info_send(0, info.at[c, y, x, z], d, partner).wait_send()
        info_send(1, info.at[c, y, x], d, partner).wait_send()
        info_send(2, info.at[c, y], d, partner).wait_send()
    for way in range(2):
        for j in range(4):
            over_x(piece_of(x, j), way, j).wait_send()
            half_over_x(x + 2, way, j).wait_send()
        for k in range(2):
            for part in far_send(k, way) + near_send(k, way, 0) + near_send(k, way, 1):
                part.wait_send()
    remote(info.at[c], info.at[c], s_ic, r_ic, partner).wait_send()
    for k in range(2):
        for h in range(2):
            for r in range(2):
                mine, away, here = weight_send(k, h, r)
                pl.when(jnp.logical_not(mine))(away.wait_send)
        for s in range(4):
            mine = wx.at[k, s, c]
            remote(mine, mine, s_c.at[k, s], r_c.at[k, s], partner).wait_send()
    for b in range(2):
        mine = jnp.logical_and(z_core == c, 2 * c + b == z)
        away = remote(
            hs.at[b], ho.at[z_half], s_h.at[b], r_h.at[z_half], place(x, z_core, y, 2 * c + b)
        )
        pl.when(jnp.logical_not(mine))(away.wait_send)
    copy_gate.wait()
    copy_up.wait()


def adam_step(weight, first, second, grad):
    first_new = beta_first * first + (1.0 - beta_first) * grad
    second_new = beta_second * second + (1.0 - beta_second) * grad * grad
    moved = weight.astype(jnp.float32) + learn_rate * first_new / (
        jnp.sqrt(second_new) + adam_floor
    )
    return (moved.astype(jnp.bfloat16), first_new, second_new)


def shards(
    tokens, seeds, fitness, gate_weight, up_weight, gate_first, up_first, gate_second, up_second
):
    width, units = gate_weight.shape
    half = units // 2
    rows = tokens.shape[0]
    tokens = tokens.T
    bf, f32, i32, i16 = jnp.bfloat16, jnp.float32, jnp.int32, jnp.int16
    vmem = pl.BlockSpec(memory_space=pltpu.VMEM)
    anywhere = pl.BlockSpec(memory_space=pl.ANY)
    dma = pltpu.SemaphoreType.DMA
    hidden, grad_gate, grad_up = pl.pallas_call(
        kernel,
        name="generation",
        out_shape=(
            jax.ShapeDtypeStruct((rows // 2, units), bf),
            jax.ShapeDtypeStruct((width, units), f32),
            jax.ShapeDtypeStruct((width, units), f32),
        ),
        in_specs=[anywhere, vmem, vmem, anywhere, anywhere],
        out_specs=(vmem, anywhere, anywhere),
        scratch_shapes=[
            pltpu.VMEM((4, 4, width, rows), bf),
            pltpu.VMEM((4, rows, 4 * width), bf),
            pltpu.VMEM((2, 4, 2, width // 2, half), bf),
            pltpu.VMEM((2, 4, 4, 4, 8, 128), f32),
            pltpu.VMEM((16, 128), i32),
            pltpu.VMEM((16, 128), f32),
            pltpu.VMEM((2, 2, 2, rows // 2, half), i16),
            pltpu.VMEM((2, 2, 2, 8, 128), f32),
            pltpu.VMEM((2, 2, 2, rows // 2, half), i16),
            pltpu.VMEM((2, 2, 2, 8, 128), f32),
            pltpu.VMEM((2, 2, rows // 2, half), i16),
            pltpu.VMEM((2, 2, 8, 128), f32),
            pltpu.VMEM((2, 2, rows // 2, half), i16),
            pltpu.VMEM((2, 2, 8, 128), f32),
            pltpu.VMEM((2, 2, rows, half), f32),
            pltpu.VMEM((2, width, MEMBERS), bf),
            pltpu.VMEM((256, MEMBERS), bf),
            pltpu.VMEM((2, width, units), f32),
            pltpu.VMEM((2, rows // 2, half), bf),
            pltpu.VMEM((2, rows // 2, half), bf),
            dma((3,)),
            dma((3,)),
            dma((2, 4)),
            dma((2, 4)),
            dma((2, 4)),
            dma((2, 4)),
            dma,
            dma((2, 4)),
            dma((2, 4)),
            dma((2, 4)),
            dma((2, 4)),
            dma((3, 3)),
            dma((3, 3)),
            dma,
            dma,
            dma((2, 2, 2)),
            dma((2, 2, 2)),
            dma((2, 2, 2)),
            dma((2, 2, 2)),
            dma((2, 2)),
            dma((2, 2)),
            dma((2, 2)),
            dma((2, 2)),
            dma((2,)),
            dma((2,)),
            dma((2,)),
        ],
        compiler_params=pltpu.CompilerParams(
            collective_id=0, has_side_effects=True, vmem_limit_bytes=56 << 20
        ),
    )(tokens, seeds.reshape(16, 128), fitness.reshape(1, 16), gate_weight, up_weight)
    gate_new, gate_first_new, gate_second_new = adam_step(
        gate_weight, gate_first, gate_second, grad_gate
    )
    up_new, up_first_new, up_second_new = adam_step(up_weight, up_first, up_second, grad_up)
    return (hidden, gate_new, up_new, gate_first_new, up_first_new, gate_second_new, up_second_new)


def solution(mesh):
    spread = P("fsdp", "pop")
    return jax.shard_map(
        shards,
        mesh=mesh,
        in_specs=(P("pop", "fsdp"), P(), P(("pop", "fsdp"))) + (spread,) * 6,
        out_specs=(spread,) * 7,
        check_vma=False,
    )
```
